256 devices in a mesh: lon: 16 (over z, x_hi), lat: 16 (over x_lo, y, core).
Axes of the slice: x: 4 (x_hi: 2, x_lo: 2; x = x_hi * 2 + x_lo), y: 4, z: 8, core: 2. Of those that a mesh axis runs over, the one named last changes fastest.
Arguments:
- thermal_departure: float32 [6, 3072, 4096], P(None, 'lat', 'lon'), may hold values from -6 to 6
- saltiness_departure: float32 [6, 3072, 4096], P(None, 'lat', 'lon'), may hold values from -6 to 6
- eastern_edge_speed: float32 [6, 3072, 4096], P(None, 'lat', 'lon'), may hold values from -3 to 3
- northern_edge_speed: float32 [6, 3072, 4096], P(None, 'lat', 'lon'), may hold values from -3 to 3
- water_land_indicator: int32 [6, 3072, 4096], P(None, 'lat', 'lon'), may hold values 0 or 1
Outputs:
- temperature_next: float32 [6, 3072, 4096], P(None, 'lat', 'lon')
- salinity_next: float32 [6, 3072, 4096], P(None, 'lat', 'lon')
- u_next: float32 [6, 3072, 4096], P(None, 'lat', 'lon')
- v_next: float32 [6, 3072, 4096], P(None, 'lat', 'lon')
The draws below stay inside these ranges and needn't reach their ends.
Inputs may be any that keep to these rules, and one draw needn't show every extreme that they name: `water_land_indicator`: 1 marks a sea cell, 0 a land cell.
All inputs are finite; a program needn't handle non-finite values. No bound on the sum of `water_land_indicator` on one device may be relied on, other than what follows from the above.
Results may differ from the reference program's by a relative error of at most 0.00002.
Values sent between devices are 32-bit elements; how exact they have to be, the bound alone decides.
A program may use at most 128 MiB of HBM per device.

```python
import jax
import jax.numpy as jnp

LAYER_NUMBER = 6
STEPS = 2
MERIDIAN_TOTAL = 4096
PARALLEL_TOTAL = 3072


def place_ends(values, own_key, low, high):
    spot = [jax.random.randint(jax.random.fold_in(own_key, axis), (), 0, length) for axis, length in enumerate(values.shape)]
    widest = values.shape.index(max(values.shape))
    beside = spot[:widest] + [(spot[widest] + 1) % values.shape[widest]] + spot[widest + 1:]
    return values.at[tuple(spot)].set(low).at[tuple(beside)].set(high)


def block_levels(key, extent, shards, least, top_value):
    def one(position, shards_of):
        heights = jax.random.uniform(jax.random.fold_in(jax.random.fold_in(key, 6), position), (shards_of,), jnp.float32, least / len(shards), top_value / len(shards))
        return jnp.repeat(jnp.exp(heights), extent[position] // shards_of).reshape((-1,) + (1,) * (len(extent) - position - 1))

    loudness = one(*shards[0])
    for cut in shards[1:]:
        loudness = loudness * one(*cut)
    return loudness


def scatter_about(key, shape, spread, limit, pieces=(), held_as=jnp.bfloat16):
    entries = jax.random.normal(key, shape, jnp.float32) * spread
    if len(pieces) > 0:
        entries = block_levels(key, shape, pieces, -0.22, 0.18) * entries
    return jnp.clip(entries, min=-limit, max=limit).astype(held_as)


def setup_inputs(seed: int = 0) -> dict:
    seeds = jax.random.split(jax.random.key(seed), 6)
    thermal_departure = scatter_about(seeds[0], (LAYER_NUMBER, PARALLEL_TOTAL, MERIDIAN_TOTAL), 1.0, 6.0, ((1, 16), (2, 16)), jnp.float32)
    saltiness_departure = scatter_about(seeds[1], (LAYER_NUMBER, PARALLEL_TOTAL, MERIDIAN_TOTAL), 1.0, 6.0, ((1, 16), (2, 16)), jnp.float32)
    eastern_edge_speed = scatter_about(seeds[2], (LAYER_NUMBER, PARALLEL_TOTAL, MERIDIAN_TOTAL), 0.5, 3.0, ((1, 16), (2, 16)), jnp.float32)
    northern_edge_speed = scatter_about(seeds[3], (LAYER_NUMBER, PARALLEL_TOTAL, MERIDIAN_TOTAL), 0.5, 3.0, ((1, 16), (2, 16)), jnp.float32)
    water_land_indicator = place_ends((jax.random.randint(seeds[4], (LAYER_NUMBER, PARALLEL_TOTAL, MERIDIAN_TOTAL), 0, 5) < 4).astype(jnp.int32), jax.random.fold_in(seeds[4], 1), 0, 1)
    return {"thermal_departure": thermal_departure, "saltiness_departure": saltiness_departure, "eastern_edge_speed": eastern_edge_speed, "northern_edge_speed": northern_edge_speed, "water_land_indicator": water_land_indicator}


time_step = 0.2


def face_flux(before, centre, after, beyond, velocity):
    return velocity * (7.0 * (centre + after) - (before + beyond)) / 12.0 - jnp.abs(velocity) * (3.0 * (after - centre) - (beyond - before)) / 12.0


def east_extend(joined_tracer_planes):
    return jnp.concatenate([joined_tracer_planes[..., -2:], joined_tracer_planes, joined_tracer_planes[..., :2]], axis=3)


def north_extend(joined_tracer_planes, parity):
    south_rows = jnp.zeros(joined_tracer_planes.shape[:2] + (2, joined_tracer_planes.shape[3]), jnp.float32)
    top_rows = jnp.stack([joined_tracer_planes[:, :, -1], joined_tracer_planes[:, :, -2]], axis=2)[..., ::-1] * parity[:, None, None, None]
    return jnp.concatenate([south_rows, joined_tracer_planes, top_rows], axis=2)


def advance(joined_tracer_planes, wet, wet_east, wet_north, parity):
    col_count = joined_tracer_planes.shape[3]
    row_count = joined_tracer_planes.shape[2]
    east = east_extend(joined_tracer_planes)
    centre = east[..., 1:col_count + 2]
    flux = face_flux(east[..., 0:col_count + 1], centre, east[..., 2:col_count + 3], east[..., 3:col_count + 4], centre[2:3])
    flux = flux * (wet_east[..., 1:col_count + 2] * wet_east[..., 2:col_count + 3])
    div_east = flux[..., 1:] - flux[..., :-1]
    north = north_extend(joined_tracer_planes, parity)
    centre = north[:, :, 1:row_count + 2]
    flux = face_flux(north[:, :, 0:row_count + 1], centre, north[:, :, 2:row_count + 3], north[:, :, 3:row_count + 4], centre[3:4])
    flux = flux * (wet_north[:, :, 1:row_count + 2] * wet_north[:, :, 2:row_count + 3])
    div_north = flux[:, :, 1:] - flux[:, :, :-1]
    return (joined_tracer_planes - time_step * (div_east + div_north)) * wet


def reference(thermal_departure, saltiness_departure, eastern_edge_speed, northern_edge_speed, water_land_indicator):
    wet = water_land_indicator.astype(jnp.float32)[None]
    wet_east = east_extend(wet)
    wet_north = north_extend(wet, jnp.ones((1,), jnp.float32))
    parity = jnp.array([1.0, 1.0, -1.0, -1.0], jnp.float32)
    joined_tracer_planes = jnp.stack([thermal_departure, saltiness_departure, eastern_edge_speed, northern_edge_speed])
    for turn in range(STEPS):
        joined_tracer_planes = advance(joined_tracer_planes, wet, wet_east, wet_north, parity)
    return (joined_tracer_planes[0], joined_tracer_planes[1], joined_tracer_planes[2], joined_tracer_planes[3])
```

```python
import functools

import jax
import jax.numpy as jnp
from jax import lax
from jax.experimental import pallas as pl
from jax.experimental.pallas import tpu as pltpu
from jax.sharding import PartitionSpec as P

MESH = pl.DeviceIdType.MESH
SCALE = 0.2 / 6.0
PITCH = 20
CHUNKS = 4


def lanes():
    return lax.broadcasted_iota(jnp.int32, (8, 128), 1)


def spot():
    return lax.rem(lax.rem(lanes() + 4, 128), PITCH)


def roll(x, shift):
    shift = shift % 128 if isinstance(shift, int) else shift
    return x if isinstance(shift, int) and shift == 0 else pltpu.roll(x, shift, 1)


def ahead(pair):
    if len(pair) == 1:
        return [roll(pair[0], 127)]
    first, second = roll(pair[0], 127), roll(pair[1], 127)
    return [jnp.where(lanes() < 127, first, second), second]


def behind(pair):
    if len(pair) == 1:
        return [roll(pair[0], 1)]
    first, second = roll(pair[0], 1), roll(pair[1], 1)
    return [first, jnp.where(lanes() > 0, second, first)]


def each(function, *pairs):
    return [function(*items) for items in zip(*pairs)]


def tripled(pair):
    return each(lambda q: 3.0 * q, pair)


def face(weight, south, here, north, beyond):
    def one(w, a, b, c, d):
        return w * (2.0 * (b + c) + jnp.where(w > 0.0, 3.0 * b - a, 3.0 * c - d))

    return each(one, weight, south, here, north, beyond)


def east_change(weight, here):
    after = ahead(here)
    low = each(lambda q, r: 3.0 * q - r, here, behind(here))
    high = ahead(each(lambda q, r: 3.0 * q - r, here, after))
    flux = each(
        lambda w, q, r, l, h: w * (2.0 * (q + r) + jnp.where(w > 0.0, l, h)), weight, here, after, low, high
    )
    return each(lambda f, g: f - g, flux, behind(flux))


def updated(here, east, north, before, wet):
    return each(lambda q, e, n, m, s: (q - (e + (n - m))) * s, here, east, north, before, wet)


def north_fluxes(load, weight, offset):
    return [
        face(weight, load(k, offset - 1), load(k, offset), load(k, offset + 1), load(k, offset + 2)) for k in range(4)
    ]


def wet_faces(load, offset, along_rows):
    here = load(4, offset)
    other = load(4, offset + 1) if along_rows else ahead(here)
    return each(lambda a, b: a * b * SCALE, here, other)


def weights(load, faces, k, offset):
    return each(lambda w, s: w * s, load(k, offset), faces)


def local_position():
    return lax.axis_index("lon"), lax.axis_index("lat")


def advance_kernel(
    lon_count,
    lat_count,
    t_ref,
    s_ref,
    u_ref,
    v_ref,
    w_ref,
    out,
    strips_out,
    x0,
    x1,
    wet_int,
    east_wet,
    north_wet,
    rows_in,
    wet_rows_in,
    packed,
    packed_next,
    wires,
    wires_in,
    strip,
    strip_mid,
    strip_next,
    load_sem,
    row_send,
    row_recv,
    wire_send,
    wire_recv,
):
    inputs = (t_ref, s_ref, u_ref, v_ref, w_ref)
    layers, rows, _ = t_ref.shape
    stride = rows // 8
    north_pad = 8 + rows
    lon, lat = local_position()
    top = lat == lat_count - 1
    bottom = lat == 0
    east = {"lon": lax.rem(lon + 1, lon_count)}
    west = {"lon": lax.rem(lon + lon_count - 1, lon_count)}
    mirror = {"lon": lon_count - 1 - lon}

    loads = []
    for k in (4, 0, 1, 2, 3):
        for half in range(2):
            here = inputs[k].at[:, :, pl.ds(128 * half, 128)]
            there = wet_int.at[:, half] if k == 4 else x0.at[k, :, half, pl.ds(8, rows)]
            loads.append(pltpu.make_async_copy(here, there, load_sem.at[k, half]))
    for copy in loads:
        copy.start()

    barrier = pltpu.get_barrier_semaphore()
    pl.semaphore_signal(barrier, inc=1, device_id=east, device_id_type=MESH)
    pl.semaphore_signal(barrier, inc=1, device_id=west, device_id_type=MESH)

    @pl.when(top)
    def _():
        pl.semaphore_signal(barrier, inc=1, device_id=mirror, device_id_type=MESH)

    @pl.when(jnp.logical_not(top))
    def _():
        pl.semaphore_signal(barrier, inc=1, device_id={"lat": lat + 1}, device_id_type=MESH)

    @pl.when(jnp.logical_not(bottom))
    def _():
        pl.semaphore_signal(barrier, inc=1, device_id={"lat": lat - 1}, device_id_type=MESH)
        pl.semaphore_wait(barrier, 4)

    @pl.when(bottom)
    def _():
        pl.semaphore_wait(barrier, 3)

    def row_copies(first, there, side, device):
        copies = []
        for k in range(5):
            for half in range(2):
                source = inputs[k].at[:, pl.ds(first, 4), pl.ds(128 * half, 128)]
                if k == 4:
                    target = wet_rows_in.at[side, :, half, pl.ds(there, 4)]
                else:
                    target = rows_in.at[side, k, :, half, pl.ds(there, 4)]
                up = 0 if first else 1
                copies.append(
                    pltpu.make_async_remote_copy(
                        source,
                        target,
                        row_send.at[up, k, half],
                        row_recv.at[side, k, half],
                        device_id=device,
                        device_id_type=MESH,
                    )
                )
        return copies

    to_north = row_copies(rows - 4, 4, 0, {"lat": jnp.minimum(lat + 1, lat_count - 1)})
    to_mirror = row_copies(rows - 4, 4, 1, mirror)
    to_south = row_copies(0, 0, 1, {"lat": jnp.maximum(lat - 1, 0)})

    @pl.when(top)
    def _():
        for copy in to_mirror:
            copy.start()

    @pl.when(jnp.logical_not(top))
    def _():
        for copy in to_north:
            copy.start()

    @pl.when(jnp.logical_not(bottom))
    def _():
        for copy in to_south:
            copy.start()

    for copy in loads:
        copy.wait()

    def pack(source):
        place = lax.rem(lanes() + 4, 128)
        total = None
        for layer in reversed(range(layers)):
            both = jnp.where(lanes() < 64, source(layer, 0), source(layer, 1))
            moved = roll(both, PITCH * layer)
            if total is None:
                total = moved
            else:
                total = jnp.where(place < PITCH * (layer + 1) - 6, moved, total)
        return jnp.where(place < 120, total, moved)

    def pack_tile(row):
        tile = pl.ds(pl.multiple_of(row, 8), 8)
        group = spot() // 4
        group_west = lax.rem(lanes(), PITCH) // 4
        east_wire = west_wire = None
        for k in range(5):
            one = pack(lambda layer, half: x0[k, layer, half, tile, :])
            packed[k, tile, :] = one
            moved = roll(one, 4 * k)
            east_wire = moved if k == 0 else jnp.where(group == k, moved, east_wire)
            west_wire = moved if k == 0 else jnp.where(group_west == k, moved, west_wire)
        wires[0, tile, :] = east_wire
        wires[1, tile, :] = west_wire

    def wire_copies(start, count, number):
        return [
            pltpu.make_async_remote_copy(
                wires.at[side, pl.ds(start, count)],
                wires_in.at[side, pl.ds(start, count)],
                wire_send.at[side, number],
                wire_recv.at[side, number],
                device_id=device,
                device_id_type=MESH,
            )
            for side, device in ((0, east), (1, west))
        ]

    wire_parts = []
    tiles = rows // 8
    for chunk in range(CHUNKS):
        low, high = tiles * chunk // CHUNKS, tiles * (chunk + 1) // CHUNKS

        @pl.loop(low, high)
        def _(i):
            row = pl.multiple_of(8 + 8 * i, 8)

            @pl.loop(0, layers)
            def _(layer):
                for half in range(2):
                    part = wet_int[layer, half, pl.ds(pl.multiple_of(8 * i, 8), 8), :]
                    x0[4, layer, half, pl.ds(row, 8), :] = part.astype(jnp.float32)

            pack_tile(row)

        copies = wire_copies(8 + 8 * low, 8 * (high - low), chunk)
        for copy in copies:
            copy.start()
        wire_parts += copies

    def whole_blocks(source, target, first_step):
        @pl.loop(0, layers)
        def _(layer):
            def wet_at(offset):
                return [x0[4, layer, half, pl.ds(offset, 8, stride=stride), :] for half in range(2)]

            def loader(t):
                def load(k, offset):
                    at = pl.ds(8 + t + offset, 8, stride=stride)
                    return [(x0 if k == 4 else source)[k, layer, half, at, :] for half in range(2)]

                return load

            def faces(load, t, offset, along_rows):
                kept = north_wet if along_rows else east_wet
                at = pl.ds(8 + t + offset, 8, stride=stride)
                if not first_step:
                    return [kept[layer, half, at, :] for half in range(2)]
                made = wet_faces(load, offset, along_rows)
                if offset == 0:
                    for half in range(2):
                        kept[layer, half, at, :] = made[half]
                return made

            start = loader(0)
            before = north_fluxes(start, weights(start, faces(start, 0, -1, True), 3, -1), -1)

            def body(t, before):
                load = loader(t)
                north = north_fluxes(load, weights(load, faces(load, t, 0, True), 3, 0), 0)
                across = weights(load, faces(load, t, 0, False), 2, 0)
                wet = wet_at(8 + t)
                for k in range(4):
                    here = load(k, 0)
                    new = updated(here, east_change(across, here), north[k], before[k], wet)
                    for half in range(2):
                        target[k, layer, half, pl.ds(8 + t, 8, stride=stride), :] = new[half]
                return north

            lax.fori_loop(0, stride, body, before)

    sublane = lax.broadcasted_iota(jnp.int32, (8, 128), 0)

    def eight_rows(source, layer, first):
        def load(k, offset):
            at = pl.ds(first + offset, 8)
            return [(x0 if k == 4 else source)[k, layer, half, at, :] for half in range(2)]

        return load

    def changed_rows(load, across_wet, north_here, north_before, folded):
        late = 1 if folded else 0
        north = north_fluxes(load, weights(load, north_here, 3, late), 0)
        before = north_fluxes(load, weights(load, north_before, 3, late - 1), -1)
        speed = ahead(load(2, 0)) if folded else load(2, 0)
        across = each(lambda w, s: w * s, speed, across_wet)
        wet = load(4, 0)
        return [
            updated(load(k, 0), east_change(across, load(k, 0)), north[k], before[k], wet) for k in range(4)
        ]

    def edge_rows(source, target, starts, first_step):
        right = jnp.logical_and(sublane >= 2, sublane < 6)

        @pl.loop(0, layers)
        def _(layer):
            for first in starts:
                load = eight_rows(source, layer, first)
                at = pl.ds(first, 8)
                if first_step:
                    across_wet = wet_faces(load, 0, False)
                    north_here = wet_faces(load, 0, True)
                    north_before = wet_faces(load, -1, True)
                    for half in range(2):
                        east_wet[layer, half, at, :] = across_wet[half]
                        north_wet[layer, half, at, :] = north_here[half]
                else:
                    across_wet = [east_wet[layer, half, at, :] for half in range(2)]
                    north_here = [north_wet[layer, half, at, :] for half in range(2)]
                    north_before = [north_wet[layer, half, pl.ds(first - 1, 8), :] for half in range(2)]
                new = changed_rows(load, across_wet, north_here, north_before, False)
                for k in range(4):
                    for half in range(2):
                        old = target[k, layer, half, at, :]
                        target[k, layer, half, at, :] = jnp.where(right, new[k][half], old)

    past_fold = jnp.logical_and(sublane >= 4, sublane < 6)

    def fold_rows():
        first = north_pad - 4
        at = pl.ds(first, 8)

        @pl.loop(0, layers)
        def _(layer):
            load = eight_rows(x0, layer, first)
            made = [wet_faces(load, 0, False), wet_faces(load, 0, True), wet_faces(load, -1, True)]
            new = changed_rows(load, *made, True)
            for k in range(4):
                for half in range(2):
                    x1[k, layer, half, at, :] = jnp.where(past_fold, new[k][half], x1[k, layer, half, at, :])

    whole_blocks(x0, x1, True)

    @pl.when(bottom)
    def _():
        @pl.loop(0, layers)
        def _(layer):
            for half in range(2):
                for k in range(5):
                    x0[k, layer, half, pl.ds(0, 8), :] = jnp.zeros((8, 128), jnp.float32)

    @pl.when(jnp.logical_not(bottom))
    def _():
        for copy in row_copies(0, 4, 0, east):
            copy.wait_recv()

        @pl.loop(0, layers)
        def _(layer):
            for half in range(2):
                for k in range(4):
                    x0[k, layer, half, pl.ds(0, 8), :] = rows_in[0, k, layer, half]
                x0[4, layer, half, pl.ds(0, 8), :] = wet_rows_in[0, layer, half].astype(jnp.float32)

    for copy in to_south:
        copy.wait_recv()

    def north_tile(k, layer, half):
        return wet_rows_in[1, layer, half].astype(jnp.float32) if k == 4 else rows_in[1, k, layer, half]

    @pl.when(jnp.logical_not(top))
    def _():
        @pl.loop(0, layers)
        def _(layer):
            for half in range(2):
                for k in range(5):
                    x0[k, layer, half, pl.ds(north_pad, 8), :] = north_tile(k, layer, half)

    @pl.when(top)
    def _():
        @pl.loop(0, layers)
        def _(layer):
            for half in range(2):
                for k in range(5):
                    flipped = jnp.take_along_axis(north_tile(k, layer, 1 - half), 127 - lanes(), axis=1)
                    if k in (2, 3):
                        flipped = -flipped
                    for row in range(4):
                        x0[k, layer, half, pl.ds(north_pad + row, 1), :] = flipped[7 - row : 8 - row, :]

    pack_tile(0)
    pack_tile(north_pad)
    for number, start in ((CHUNKS, 0), (CHUNKS + 1, north_pad)):
        copies = wire_copies(start, 8, number)
        for copy in copies:
            copy.start()
        wire_parts += copies

    edge_rows(x0, x1, (4, north_pad - 4), True)
    pl.when(top)(fold_rows)
    whole_blocks(x1, out, False)
    edge_rows(x1, out, (6, north_pad - 6), False)

    @pl.loop(0, tiles + 2)
    def _(i):
        tile = pl.ds(pl.multiple_of(8 * i, 8), 8)
        for k in range(5):
            source = x0 if k == 4 else x1
            packed_next[k, tile, :] = pack(lambda layer, half: source[k, layer, half, tile, :])

    for copy in wire_parts:
        copy.wait_recv()

    @pl.loop(0, tiles + 2)
    def _(i):
        tile = pl.ds(pl.multiple_of(8 * i, 8), 8)
        place = spot()
        for k in range(5):
            own = packed[k, tile, :]
            left = jnp.where(place < 4, roll(wires_in[0, tile, :], -4 * k), own)
            right = jnp.where(place < 4, own, roll(wires_in[1, tile, :], -4 * k))
            strip[k, tile, :] = jnp.where(place < 8, left, roll(right, 8))

    def strip_step(source, start, count, put):
        def loader(t):
            def load(k, offset):
                return [source[k, pl.ds(start + t + offset, 8, stride=stride), :]]

            return load

        first = loader(0)
        before = north_fluxes(first, weights(first, wet_faces(first, -1, True), 3, -1), -1)

        def body(t, before):
            load = loader(t)
            north = north_fluxes(load, weights(load, wet_faces(load, 0, True), 3, 0), 0)
            across = weights(load, wet_faces(load, 0, False), 2, 0)
            wet = load(4, 0)
            for k in range(4):
                here = load(k, 0)
                put(k, t, updated(here, east_change(across, here), north[k], before[k], wet)[0])
            return north

        lax.fori_loop(0, count, body, before)

    def put_mid(k, t, value):
        strip_mid[k, pl.ds(6 + t, 8, stride=stride), :] = value

    strip_step(strip, 6, stride + 4, put_mid)

    @pl.when(top)
    def _():
        first = north_pad - 4

        def load(k, offset):
            return [strip[k, pl.ds(first + offset, 8), :]]

        made = [wet_faces(load, 0, False), wet_faces(load, 0, True), wet_faces(load, -1, True)]
        new = changed_rows(load, *made, True)
        for k in range(4):
            at = pl.ds(first, 8)
            strip_mid[k, at, :] = jnp.where(past_fold, new[k][0], strip_mid[k, at, :])

    @pl.loop(0, tiles + 2)
    def _(i):
        tile = pl.ds(pl.multiple_of(8 * i, 8), 8)
        place = spot()
        for k in range(5):
            outer = strip[4, tile, :] if k == 4 else strip_mid[k, tile, :]
            inner = packed_next[k, tile, :]
            left = jnp.where(place < 4, roll(outer, -2), roll(inner, -2))
            right = jnp.where(place < 12, roll(inner, 10), roll(outer, 2))
            strip_next[k, tile, :] = jnp.where(place < 8, left, right)

    def put_out(k, t, value):
        place = spot()
        inside = jnp.logical_and(place >= 2, place < 6)
        strips_out[k, pl.ds(t, 8, stride=stride), :] = jnp.where(inside, value, roll(value, -12))

    strip_step(strip_next, 8, stride, put_out)

    for copy in wire_parts:
        copy.wait_send()
    for copy in to_mirror:
        copy.wait_send()

    @pl.when(jnp.logical_not(bottom))
    def _():
        for copy in to_south:
            copy.wait_send()


def write_kernel(blocks, strips, t_out, s_out, u_out, v_out, whole, sem):
    layers, rows, _ = t_out.shape
    copies = []
    for k, output in enumerate((t_out, s_out, u_out, v_out)):
        for layer in range(layers):

            @pl.loop(0, rows // 8)
            def _(i):
                start = pl.multiple_of(8 * i, 8)
                moved = roll(strips[k, pl.ds(start, 8), :], (2 - PITCH * layer) % 128)
                for half in range(2):
                    edge = lanes() < 4 if half == 0 else lanes() >= 124
                    block = blocks[k, layer, half, pl.ds(start + 8, 8), :]
                    whole[k, layer, half, pl.ds(start, 8), :] = jnp.where(edge, moved, block)

            for half in range(2):
                there = output.at[layer, :, pl.ds(128 * half, 128)]
                copy = pltpu.make_async_copy(whole.at[k, layer, half], there, sem.at[k, layer, half])
                copy.start()
                copies.append(copy)
    for copy in copies:
        copy.wait()


def local(lon_count, lat_count, *arrays):
    layers, rows, columns = arrays[0].shape
    padded = rows + 16
    vmem = pl.BlockSpec(memory_space=pltpu.VMEM)
    anywhere = pl.BlockSpec(memory_space=pltpu.HBM)
    dma = pltpu.SemaphoreType.DMA
    f32 = jnp.float32
    blocks, strips = pl.pallas_call(
        functools.partial(advance_kernel, lon_count, lat_count),
        name="advance",
        out_shape=(
            jax.ShapeDtypeStruct((4, layers, 2, padded, 128), f32),
            jax.ShapeDtypeStruct((4, rows, 128), f32),
        ),
        in_specs=[anywhere] * 5,
        out_specs=(vmem, vmem),
        scratch_shapes=[
            pltpu.VMEM((5, layers, 2, padded, 128), f32),
            pltpu.VMEM((4, layers, 2, padded, 128), f32),
            pltpu.VMEM((layers, 2, rows, 128), jnp.int32),
            pltpu.VMEM((layers, 2, padded, 128), f32),
            pltpu.VMEM((layers, 2, padded, 128), f32),
            pltpu.VMEM((2, 4, layers, 2, 8, 128), f32),
            pltpu.VMEM((2, layers, 2, 8, 128), jnp.int32),
            pltpu.VMEM((5, padded, 128), f32),
            pltpu.VMEM((5, padded, 128), f32),
            pltpu.VMEM((2, padded, 128), f32),
            pltpu.VMEM((2, padded, 128), f32),
            pltpu.VMEM((5, padded, 128), f32),
            pltpu.VMEM((4, padded, 128), f32),
            pltpu.VMEM((5, padded, 128), f32),
            dma((5, 2)),
            dma((2, 5, 2)),
            dma((2, 5, 2)),
            dma((2, CHUNKS + 2)),
            dma((2, CHUNKS + 2)),
        ],
        compiler_params=pltpu.CompilerParams(collective_id=0, has_side_effects=True, vmem_limit_bytes=40 << 20),
    )(*(pltpu.with_memory_space_constraint(array, pltpu.HBM) for array in arrays))
    return pl.pallas_call(
        write_kernel,
        name="write",
        out_shape=tuple(jax.ShapeDtypeStruct((layers, rows, columns), f32) for _ in range(4)),
        in_specs=[vmem, vmem],
        out_specs=(anywhere,) * 4,
        scratch_shapes=[pltpu.VMEM((4, layers, 2, rows, 128), f32), dma((4, layers, 2))],
        compiler_params=pltpu.CompilerParams(vmem_limit_bytes=40 << 20),
    )(blocks, strips)


def solution(mesh):
    placed = P(None, "lat", "lon")
    return jax.shard_map(
        functools.partial(local, mesh.shape["lon"], mesh.shape["lat"]),
        mesh=mesh,
        in_specs=(placed,) * 5,
        out_specs=(placed,) * 4,
        check_vma=False,
    )
```

```python
import functools

import jax
import jax.numpy as jnp
from jax import lax
from jax.experimental import pallas as pl
from jax.experimental.pallas import tpu as pltpu
from jax.sharding import PartitionSpec as P

MESH = pl.DeviceIdType.MESH
SCALE = 0.2 / 6.0
PITCH = 20
CHUNKS = 4
WRITTEN = 6
PACKED = 2
EDGES = 3
BLOCKS = 6
STRIPS = 5


def lanes():
    return lax.broadcasted_iota(jnp.int32, (8, 128), 1)


def spot():
    return lax.rem(lax.rem(lanes() + 4, 128), PITCH)


def roll(x, shift):
    shift = shift % 128 if isinstance(shift, int) else shift
    return x if isinstance(shift, int) and shift == 0 else pltpu.roll(x, shift, 1)


def shifted(values, distance):
    moved = [roll(value, -distance) for value in values]
    if len(moved) == 1:
        return moved
    first, second = moved
    if distance > 0:
        return [jnp.where(lanes() < 128 - distance, first, second), second]
    return [first, jnp.where(lanes() >= -distance, second, first)]


def face(weight, positive, before, here, after, beyond):
    return weight * (2.0 * (here + after) + jnp.where(positive, 3.0 * here - before, 3.0 * after - beyond))


def fluxes(weight, fields):
    positive = [w > 0.0 for w in weight]
    return [[face(*values) for values in zip(weight, positive, *field)] for field in fields]


def tiles_step(tiles):
    across = []
    for load, _, _, _, _ in tiles:
        here = [load(k, 0) for k in range(4)]
        across.append([(shifted(q, -1), q, shifted(q, 1), shifted(q, 2)) for q in here])
    weights = []
    for (load, faces, _, _, late), fields in zip(tiles, across):
        east_wet, north_wet = faces()
        u = fields[2][2] if late else fields[2][1]
        v = load(3, 1) if late else fields[3][1]
        weights.append(([q * s for q, s in zip(u, east_wet)], [q * s for q, s in zip(v, north_wet)]))
    east = []
    for fields, (weight, _) in zip(across, weights):
        flux = fluxes(weight, fields)
        east.append([(f, shifted(f, -1)) for f in flux])
    for (load, _, south, put, _), fields, (_, weight), changes in zip(tiles, across, weights, east):
        wet = load(4, 0)
        north = fluxes(weight, [(load(k, -1), fields[k][1], load(k, 1), load(k, 2)) for k in range(4)])
        for k in range(4):
            flux, west = changes[k]
            parts = zip(fields[k][1], flux, west, north[k], south(k, north[k]), wet)
            put(k, [(q - ((e - w) + (n - m))) * s for q, e, w, n, m, s in parts])


def rolled_south(k, flux):
    return [pltpu.roll(value, 1, 0) for value in flux]


def wet_faces(load):
    here = load(4, 0)
    pairs = zip(here, shifted(here, 1), load(4, 1))
    made = [(w * e * SCALE, w * n * SCALE) for w, e, n in pairs]
    return [m[0] for m in made], [m[1] for m in made]


def local_position():
    return lax.axis_index("lon"), lax.axis_index("lat")


def advance_kernel(
    lon_count,
    lat_count,
    t_ref,
    s_ref,
    u_ref,
    v_ref,
    w_ref,
    out,
    strips_out,
    x0,
    x1,
    wet_int,
    east_wet,
    north_wet,
    rows_in,
    wet_rows_in,
    packed,
    packed_next,
    wires,
    wires_in,
    strip,
    strip_mid,
    strip_next,
    flows,
    strip_flows,
    load_sem,
    row_send,
    row_recv,
    wire_send,
    wire_recv,
):
    inputs = (t_ref, s_ref, u_ref, v_ref, w_ref)
    layers, rows, _ = t_ref.shape
    north_pad = 8 + rows
    lon, lat = local_position()
    top = lat == lat_count - 1
    bottom = lat == 0
    east = {"lon": lax.rem(lon + 1, lon_count)}
    west = {"lon": lax.rem(lon + lon_count - 1, lon_count)}
    mirror = {"lon": lon_count - 1 - lon}

    loads = []
    for k in (4, 0, 1, 2, 3):
        for half in range(2):
            here = inputs[k].at[:, :, pl.ds(128 * half, 128)]
            there = wet_int.at[:, half] if k == 4 else x0.at[k, :, half, pl.ds(8, rows)]
            loads.append(pltpu.make_async_copy(here, there, load_sem.at[k, half]))
    for copy in loads:
        copy.start()

    barrier = pltpu.get_barrier_semaphore()
    pl.semaphore_signal(barrier, inc=1, device_id=east, device_id_type=MESH)
    pl.semaphore_signal(barrier, inc=1, device_id=west, device_id_type=MESH)

    @pl.when(top)
    def _():
        pl.semaphore_signal(barrier, inc=1, device_id=mirror, device_id_type=MESH)

    @pl.when(jnp.logical_not(top))
    def _():
        pl.semaphore_signal(barrier, inc=1, device_id={"lat": lat + 1}, device_id_type=MESH)

    @pl.when(jnp.logical_not(bottom))
    def _():
        pl.semaphore_signal(barrier, inc=1, device_id={"lat": lat - 1}, device_id_type=MESH)
        pl.semaphore_wait(barrier, 4)

    @pl.when(bottom)
    def _():
        pl.semaphore_wait(barrier, 3)

    def row_copies(first, there, side, device):
        copies = []
        for k in range(5):
            for half in range(2):
                source = inputs[k].at[:, pl.ds(first, 4), pl.ds(128 * half, 128)]
                if k == 4:
                    target = wet_rows_in.at[side, :, half, pl.ds(there, 4)]
                else:
                    target = rows_in.at[side, k, :, half, pl.ds(there, 4)]
                up = 0 if first else 1
                copies.append(
                    pltpu.make_async_remote_copy(
                        source,
                        target,
                        row_send.at[up, k, half],
                        row_recv.at[side, k, half],
                        device_id=device,
                        device_id_type=MESH,
                    )
                )
        return copies

    to_north = row_copies(rows - 4, 4, 0, {"lat": jnp.minimum(lat + 1, lat_count - 1)})
    to_mirror = row_copies(rows - 4, 4, 1, mirror)
    to_south = row_copies(0, 0, 1, {"lat": jnp.maximum(lat - 1, 0)})

    @pl.when(top)
    def _():
        for copy in to_mirror:
            copy.start()

    @pl.when(jnp.logical_not(top))
    def _():
        for copy in to_north:
            copy.start()

    @pl.when(jnp.logical_not(bottom))
    def _():
        for copy in to_south:
            copy.start()

    for copy in loads:
        copy.wait()

    def pack(source):
        place = lax.rem(lanes() + 4, 128)
        total = None
        for layer in reversed(range(layers)):
            both = jnp.where(lanes() < 64, source(layer, 0), source(layer, 1))
            moved = roll(both, PITCH * layer)
            if total is None:
                total = moved
            else:
                total = jnp.where(place < PITCH * (layer + 1) - 6, moved, total)
        return jnp.where(place < 120, total, moved)

    def pack_tiles(starts):
        group = spot() // 4
        group_west = lax.rem(lanes(), PITCH) // 4
        own = []
        for row in starts:
            tile = pl.ds(row, 8)
            own.append([pack(lambda layer, half: x0[k, layer, half, tile, :]) for k in range(5)])
        moved = [[roll(one, 4 * k) for k, one in enumerate(ones)] for ones in own]
        for row, ones, others in zip(starts, own, moved):
            tile = pl.ds(row, 8)
            east_wire, west_wire = others[0], others[0]
            for k in range(5):
                packed[k, tile, :] = ones[k]
                east_wire = jnp.where(group == k, others[k], east_wire)
                west_wire = jnp.where(group_west == k, others[k], west_wire)
            wires[0, tile, :] = east_wire
            wires[1, tile, :] = west_wire

    def wire_copies(start, count, number):
        return [
            pltpu.make_async_remote_copy(
                wires.at[side, pl.ds(start, count)],
                wires_in.at[side, pl.ds(start, count)],
                wire_send.at[side, number],
                wire_recv.at[side, number],
                device_id=device,
                device_id_type=MESH,
            )
            for side, device in ((0, east), (1, west))
        ]

    wire_parts = []
    tiles = rows // 8
    for chunk in range(CHUNKS):
        low, high = tiles * chunk // CHUNKS, tiles * (chunk + 1) // CHUNKS

        @pl.loop(0, (high - low) // PACKED)
        def _(i):
            first = pl.multiple_of(8 * (low + PACKED * i), 8)
            for layer in range(layers):
                for half in range(2):
                    part = wet_int[layer, half, pl.ds(first, 8 * PACKED), :]
                    x0[4, layer, half, pl.ds(first + 8, 8 * PACKED), :] = part.astype(jnp.float32)
            pack_tiles([pl.multiple_of(first + 8 + 8 * j, 8) for j in range(PACKED)])

        copies = wire_copies(8 + 8 * low, 8 * (high - low), chunk)
        for copy in copies:
            copy.start()
        wire_parts += copies

    def loader(source, layer, first):
        def load(k, offset):
            at = pl.ds(first + offset, 8)
            return [(x0 if k == 4 else source)[k, layer, half, at, :] for half in range(2)]

        return load

    def face_weights(load, layer, first, first_step):
        def faces():
            at = pl.ds(first, 8)
            if not first_step:
                return tuple([kept[layer, half, at, :] for half in range(2)] for kept in (east_wet, north_wet))
            made = wet_faces(load)
            for kept, parts in zip((east_wet, north_wet), made):
                for half in range(2):
                    kept[layer, half, at, :] = parts[half]
            return made

        return faces

    def whole_blocks(source, target, first_step):
        def tile(layer, first):
            at = pl.ds(first, 8)

            def south(k, flux):
                for half in range(2):
                    flows[k, half, at, :] = flux[half]
                return [flows[k, half, pl.ds(first - 1, 8), :] for half in range(2)]

            def put(k, new):
                for half in range(2):
                    target[k, layer, half, at, :] = new[half]

            load = loader(source, layer, first)
            return load, face_weights(load, layer, first, first_step), south, put, False

        @pl.loop(0, layers)
        def _(layer):
            @pl.loop(0, rows // (8 * BLOCKS))
            def _(i):
                first = pl.multiple_of(8 + 8 * BLOCKS * i, 8)
                tiles_step([tile(layer, first + 8 * j) for j in range(BLOCKS)])

    sublane = lax.broadcasted_iota(jnp.int32, (8, 128), 0)

    def edge_rows(source, target, first, first_step):
        right = jnp.logical_and(sublane >= 2, sublane < 6)

        def tile(layer):
            at = pl.ds(first, 8)

            def put(k, new):
                for half in range(2):
                    target[k, layer, half, at, :] = jnp.where(right, new[half], target[k, layer, half, at, :])

            load = loader(source, layer, first)
            return load, face_weights(load, layer, first, first_step), rolled_south, put, False

        @pl.loop(0, layers // EDGES)
        def _(i):
            tiles_step([tile(EDGES * i + j) for j in range(EDGES)])

    past_fold = jnp.logical_and(sublane >= 4, sublane < 6)

    def fold_rows():
        first = north_pad - 4

        def tile(layer):
            at = pl.ds(first, 8)

            def put(k, new):
                for half in range(2):
                    x1[k, layer, half, at, :] = jnp.where(past_fold, new[half], x1[k, layer, half, at, :])

            load = loader(x0, layer, first)
            return load, lambda: wet_faces(load), rolled_south, put, True

        @pl.loop(0, layers // EDGES)
        def _(i):
            tiles_step([tile(EDGES * i + j) for j in range(EDGES)])

    whole_blocks(x0, x1, True)

    @pl.when(bottom)
    def _():
        @pl.loop(0, layers)
        def _(layer):
            for half in range(2):
                for k in range(5):
                    x0[k, layer, half, pl.ds(0, 8), :] = jnp.zeros((8, 128), jnp.float32)

    @pl.when(jnp.logical_not(bottom))
    def _():
        for copy in row_copies(0, 4, 0, east):
            copy.wait_recv()

        @pl.loop(0, layers)
        def _(layer):
            for half in range(2):
                for k in range(4):
                    x0[k, layer, half, pl.ds(0, 8), :] = rows_in[0, k, layer, half]
                x0[4, layer, half, pl.ds(0, 8), :] = wet_rows_in[0, layer, half].astype(jnp.float32)

    for copy in to_south:
        copy.wait_recv()

    def north_tile(k, layer, half):
        return wet_rows_in[1, layer, half].astype(jnp.float32) if k == 4 else rows_in[1, k, layer, half]

    @pl.when(jnp.logical_not(top))
    def _():
        @pl.loop(0, layers)
        def _(layer):
            for half in range(2):
                for k in range(5):
                    x0[k, layer, half, pl.ds(north_pad, 8), :] = north_tile(k, layer, half)

    @pl.when(top)
    def _():
        @pl.loop(0, layers)
        def _(layer):
            for half in range(2):
                for k in range(5):
                    flipped = jnp.take_along_axis(north_tile(k, layer, 1 - half), 127 - lanes(), axis=1)
                    if k in (2, 3):
                        flipped = -flipped
                    for row in range(4):
                        x0[k, layer, half, pl.ds(north_pad + row, 1), :] = flipped[7 - row : 8 - row, :]

    pack_tiles([0, north_pad])
    for number, start in ((CHUNKS, 0), (CHUNKS + 1, north_pad)):
        copies = wire_copies(start, 8, number)
        for copy in copies:
            copy.start()
        wire_parts += copies

    edge_rows(x0, x1, 4, True)
    edge_rows(x0, x1, north_pad - 4, True)
    pl.when(top)(fold_rows)
    whole_blocks(x1, out, False)
    edge_rows(x1, out, 6, False)
    edge_rows(x1, out, north_pad - 6, False)

    def every_tile(function):
        @pl.loop(0, (tiles + 2) // 2)
        def _(i):
            function([pl.ds(pl.multiple_of(16 * i + 8 * j, 8), 8) for j in range(2)])

    def pack_next(at):
        for tile in at:
            for k in range(5):
                source = x0 if k == 4 else x1
                packed_next[k, tile, :] = pack(lambda layer, half: source[k, layer, half, tile, :])

    every_tile(pack_next)

    for copy in wire_parts:
        copy.wait_recv()

    def join(at):
        place = spot()
        parts = []
        for tile in at:
            from_west, from_east = wires_in[0, tile, :], wires_in[1, tile, :]
            for k in range(5):
                own = packed[k, tile, :]
                parts.append((tile, k, roll(from_west, -4 * k), own, roll(own, 8), roll(from_east, 8 - 4 * k)))
        for tile, k, west_halo, west_edge, east_edge, east_halo in parts:
            left = jnp.where(place < 4, west_halo, west_edge)
            right = jnp.where(place < 12, east_edge, east_halo)
            strip[k, tile, :] = jnp.where(place < 8, left, right)

    every_tile(join)

    def strip_tile(source, first, put, south=None, late=False):
        def load(k, offset):
            return [source[k, pl.ds(first + offset, 8), :]]

        def stored(k, flux):
            strip_flows[k, pl.ds(first, 8), :] = flux[0]
            return [strip_flows[k, pl.ds(first - 1, 8), :]]

        return load, lambda: wet_faces(load), south or stored, functools.partial(put, first), late

    def strip_step(source, put):
        @pl.loop(0, (tiles + 1) // STRIPS)
        def _(i):
            first = 4 + 8 * STRIPS * i
            tiles_step([strip_tile(source, first + 8 * j, put) for j in range(STRIPS)])

    def put_mid(first, k, new):
        strip_mid[k, pl.ds(first, 8), :] = new[0]

    strip_step(strip, put_mid)

    @pl.when(top)
    def _():
        def put(first, k, new):
            at = pl.ds(first, 8)
            strip_mid[k, at, :] = jnp.where(past_fold, new[0], strip_mid[k, at, :])

        tiles_step([strip_tile(strip, north_pad - 4, put, rolled_south, True)])

    def join_next(at):
        place = spot()
        parts = []
        for tile in at:
            for k in range(5):
                outer = strip[4, tile, :] if k == 4 else strip_mid[k, tile, :]
                inner = packed_next[k, tile, :]
                parts.append((tile, k, roll(outer, -2), roll(inner, -2), roll(inner, 10), roll(outer, 2)))
        for tile, k, west_outer, west_inner, east_inner, east_outer in parts:
            left = jnp.where(place < 4, west_outer, west_inner)
            right = jnp.where(place < 12, east_inner, east_outer)
            strip_next[k, tile, :] = jnp.where(place < 8, left, right)

    every_tile(join_next)

    def put_out(first, k, new):
        place = spot()
        inside = jnp.logical_and(place >= 2, place < 6)
        strips_out[k, pl.ds(first, 8), :] = jnp.where(inside, new[0], roll(new[0], -12))

    strip_step(strip_next, put_out)

    for copy in wire_parts:
        copy.wait_send()
    for copy in to_mirror:
        copy.wait_send()

    @pl.when(jnp.logical_not(bottom))
    def _():
        for copy in to_south:
            copy.wait_send()


def write_kernel(blocks, strips, t_out, s_out, u_out, v_out, whole, sem):
    layers, rows, _ = t_out.shape
    copies = []
    for k, output in enumerate((t_out, s_out, u_out, v_out)):

        @pl.loop(0, rows // (8 * WRITTEN))
        def _(i):
            first = pl.multiple_of(8 * WRITTEN * i, 8)
            starts = [pl.multiple_of(first + 8 * j, 8) for j in range(WRITTEN)]
            strip = [strips[k, pl.ds(start + 8, 8), :] for start in starts]
            moved = [[roll(value, 2 - PITCH * layer) for layer in range(layers)] for value in strip]
            for start, values in zip(starts, moved):
                for layer in range(layers):
                    for half in range(2):
                        edge = lanes() < 4 if half == 0 else lanes() >= 124
                        block = blocks[k, layer, half, pl.ds(start + 8, 8), :]
                        whole[k, layer, half, pl.ds(start, 8), :] = jnp.where(edge, values[layer], block)

        for layer in range(layers):
            for half in range(2):
                there = output.at[layer, :, pl.ds(128 * half, 128)]
                copy = pltpu.make_async_copy(whole.at[k, layer, half], there, sem.at[k, layer, half])
                copy.start()
                copies.append(copy)
    for copy in copies:
        copy.wait()


def local(lon_count, lat_count, *arrays):
    layers, rows, columns = arrays[0].shape
    padded = rows + 16
    vmem = pl.BlockSpec(memory_space=pltpu.VMEM)
    anywhere = pl.BlockSpec(memory_space=pltpu.HBM)
    dma = pltpu.SemaphoreType.DMA
    f32 = jnp.float32
    blocks, strips = pl.pallas_call(
        functools.partial(advance_kernel, lon_count, lat_count),
        name="advance",
        out_shape=(
            jax.ShapeDtypeStruct((4, layers, 2, padded, 128), f32),
            jax.ShapeDtypeStruct((4, padded, 128), f32),
        ),
        in_specs=[anywhere] * 5,
        out_specs=(vmem, vmem),
        scratch_shapes=[
            pltpu.VMEM((5, layers, 2, padded, 128), f32),
            pltpu.VMEM((4, layers, 2, padded, 128), f32),
            pltpu.VMEM((layers, 2, rows, 128), jnp.int32),
            pltpu.VMEM((layers, 2, padded, 128), f32),
            pltpu.VMEM((layers, 2, padded, 128), f32),
            pltpu.VMEM((2, 4, layers, 2, 8, 128), f32),
            pltpu.VMEM((2, layers, 2, 8, 128), jnp.int32),
            pltpu.VMEM((5, padded, 128), f32),
            pltpu.VMEM((5, padded, 128), f32),
            pltpu.VMEM((2, padded, 128), f32),
            pltpu.VMEM((2, padded, 128), f32),
            pltpu.VMEM((5, padded, 128), f32),
            pltpu.VMEM((4, padded, 128), f32),
            pltpu.VMEM((5, padded, 128), f32),
            pltpu.VMEM((4, 2, padded, 128), f32),
            pltpu.VMEM((4, padded, 128), f32),
            dma((5, 2)),
            dma((2, 5, 2)),
            dma((2, 5, 2)),
            dma((2, CHUNKS + 2)),
            dma((2, CHUNKS + 2)),
        ],
        compiler_params=pltpu.CompilerParams(collective_id=0, has_side_effects=True, vmem_limit_bytes=40 << 20),
    )(*(pltpu.with_memory_space_constraint(array, pltpu.HBM) for array in arrays))
    return pl.pallas_call(
        write_kernel,
        name="write",
        out_shape=tuple(jax.ShapeDtypeStruct((layers, rows, columns), f32) for _ in range(4)),
        in_specs=[vmem, vmem],
        out_specs=(anywhere,) * 4,
        scratch_shapes=[pltpu.VMEM((4, layers, 2, rows, 128), f32), dma((4, layers, 2))],
        compiler_params=pltpu.CompilerParams(vmem_limit_bytes=40 << 20),
    )(blocks, strips)


def solution(mesh):
    placed = P(None, "lat", "lon")
    return jax.shard_map(
        functools.partial(local, mesh.shape["lon"], mesh.shape["lat"]),
        mesh=mesh,
        in_specs=(placed,) * 5,
        out_specs=(placed,) * 4,
        check_vma=False,
    )
```

```python
import functools

import jax
import jax.numpy as jnp
from jax import lax
from jax.experimental import pallas as pl
from jax.experimental.pallas import tpu as pltpu
from jax.sharding import PartitionSpec as P

MESH = pl.DeviceIdType.MESH
SCALE = 0.2 / 6.0
PITCH = 20
CHUNKS = 4
EARLY = 2
MIDDLE = 4
BLOCKS = 12
EDGES = 6
STRIPS = 25
JOINED = 13
WRITTEN = 12


def lanes():
    return lax.broadcasted_iota(jnp.int32, (8, 128), 1)


def spot():
    return lax.rem(lax.rem(lanes() + 4, 128), PITCH)


def roll(x, shift):
    shift = shift % 128 if isinstance(shift, int) else shift
    return x if isinstance(shift, int) and shift == 0 else pltpu.roll(x, shift, 1)


def shifted(values, distance):
    moved = [roll(value, -distance) for value in values]
    if len(moved) == 1:
        return moved
    first, second = moved
    if distance > 0:
        return [jnp.where(lanes() < 128 - distance, first, second), second]
    return [first, jnp.where(lanes() >= -distance, second, first)]


def face(weight, positive, before, here, after, beyond):
    near = jnp.where(positive, here, after)
    far = jnp.where(positive, before, beyond)
    return weight * (2.0 * (here + after) + (3.0 * near - far))


def staggered(items, stages, lag):
    held = [None] * len(items)
    for step in range(len(items) + lag * (len(stages) - 1)):
        for number, stage in enumerate(stages):
            at = step - lag * number
            if 0 <= at < len(items):
                held[at] = stage(items[at], held[at])


def tiles_step(tiles, lag):
    made = {}

    def shifts(item, _):
        number, k = item
        load, east_faces, _, _, _, late = tiles[number]
        here = load(k, 0)
        fields = shifted(here, -1), here, shifted(here, 1), shifted(here, 2)
        if k == 0:
            made[number, 0] = east_faces()
        if k == 2:
            made[number, 2] = fields[2] if late else here
        return fields

    def east(item, fields):
        number, k = item
        if k == 0:
            weight = [q * s for q, s in zip(made[number, 2], made[number, 0])]
            made[number, 0] = weight, [q > 0.0 for q in weight]
        flux = [face(*values) for values in zip(*made[number, 0], *fields)]
        return flux, shifted(flux, -1)

    def north(item, changes):
        number, k = item
        load, _, north_faces, south, put, late = tiles[number]
        if k == 0:
            weight = [q * s for q, s in zip(load(3, 1 if late else 0), north_faces())]
            made[number, 0] = weight, [q > 0.0 for q in weight]
        here = load(k, 0)
        flux = [face(*values) for values in zip(*made[number, 0], load(k, -1), here, load(k, 1), load(k, 2))]
        parts = zip(here, *changes, flux, south(k, flux), load(4, 0))
        put(k, [(q - ((e - w) + (n - m))) * s for q, e, w, n, m, s in parts])

    staggered([(number, k) for number in range(len(tiles)) for k in range(4)], (shifts, east, north), lag)


def rolled_south(k, flux):
    return [pltpu.roll(value, 1, 0) for value in flux]


def wet_east(load):
    here = load(4, 0)
    return [w * e * SCALE for w, e in zip(here, shifted(here, 1))]


def wet_north(load):
    return [w * n * SCALE for w, n in zip(load(4, 0), load(4, 1))]


def local_position():
    return lax.axis_index("lon"), lax.axis_index("lat")


def advance_kernel(
    lon_count,
    lat_count,
    t_ref,
    s_ref,
    u_ref,
    v_ref,
    w_ref,
    out,
    strips_out,
    x0,
    x1,
    wet_int,
    east_wet,
    north_wet,
    rows_in,
    wet_rows_in,
    packed,
    packed_next,
    wires,
    wires_in,
    strip,
    strip_mid,
    strip_next,
    flows,
    strip_flows,
    load_sem,
    row_send,
    row_recv,
    wire_send,
    wire_recv,
):
    inputs = (t_ref, s_ref, u_ref, v_ref, w_ref)
    layers, rows, _ = t_ref.shape
    north_pad = 8 + rows
    lon, lat = local_position()
    top = lat == lat_count - 1
    bottom = lat == 0
    east = {"lon": lax.rem(lon + 1, lon_count)}
    west = {"lon": lax.rem(lon + lon_count - 1, lon_count)}
    mirror = {"lon": lon_count - 1 - lon}

    part = rows // CHUNKS

    def loads(chunk):
        first = pl.multiple_of(part * chunk, 8)
        copies = []
        for k in (4, 0, 1, 2, 3):
            for half in range(2):
                here = inputs[k].at[:, pl.ds(first, part), pl.ds(128 * half, 128)]
                if k == 4:
                    there = wet_int.at[:, half, pl.ds(first, part)]
                else:
                    there = x0.at[k, :, half, pl.ds(pl.multiple_of(first + 8, 8), part)]
                copies.append(pltpu.make_async_copy(here, there, load_sem.at[chunk, k, half]))
        return copies

    @pl.loop(0, CHUNKS)
    def _(chunk):
        for copy in loads(chunk):
            copy.start()

    barrier = pltpu.get_barrier_semaphore()
    pl.semaphore_signal(barrier, inc=1, device_id=east, device_id_type=MESH)
    pl.semaphore_signal(barrier, inc=1, device_id=west, device_id_type=MESH)

    @pl.when(top)
    def _():
        pl.semaphore_signal(barrier, inc=1, device_id=mirror, device_id_type=MESH)

    @pl.when(jnp.logical_not(top))
    def _():
        pl.semaphore_signal(barrier, inc=1, device_id={"lat": lat + 1}, device_id_type=MESH)

    @pl.when(jnp.logical_not(bottom))
    def _():
        pl.semaphore_signal(barrier, inc=1, device_id={"lat": lat - 1}, device_id_type=MESH)

    def row_copies(first, there, side, device):
        copies = []
        for k in range(5):
            for half in range(2):
                source = inputs[k].at[:, pl.ds(first, 4), pl.ds(128 * half, 128)]
                if k == 4:
                    target = wet_rows_in.at[side, :, half, pl.ds(there, 4)]
                else:
                    target = rows_in.at[side, k, :, half, pl.ds(there, 4)]
                up = 0 if first else 1
                copies.append(
                    pltpu.make_async_remote_copy(
                        source,
                        target,
                        row_send.at[up, k, half],
                        row_recv.at[side, k, half],
                        device_id=device,
                        device_id_type=MESH,
                    )
                )
        return copies

    to_north = row_copies(rows - 4, 4, 0, {"lat": jnp.minimum(lat + 1, lat_count - 1)})
    to_mirror = row_copies(rows - 4, 4, 1, mirror)
    to_south = row_copies(0, 0, 1, {"lat": jnp.maximum(lat - 1, 0)})

    def pack_moves(source):
        return [roll(jnp.where(lanes() < 64, source(layer, 0), source(layer, 1)), PITCH * layer) for layer in range(layers)]

    def pack(moves):
        place = lax.rem(lanes() + 4, 128)
        total = moves[-1]
        for layer in reversed(range(layers - 1)):
            total = jnp.where(place < PITCH * (layer + 1) - 6, moves[layer], total)
        return jnp.where(place < 120, total, moves[0])

    def pack_tiles(starts):
        group = spot() // 4
        group_west = lax.rem(lanes(), PITCH) // 4
        made = {}

        def move(item, _):
            row, k = item
            return pack_moves(lambda layer, half: x0[k, layer, half, pl.ds(row, 8), :])

        def merge(item, moves):
            row, k = item
            one = pack(moves)
            packed[k, pl.ds(row, 8), :] = one
            return roll(one, 4 * k)

        def send(item, moved):
            row, k = item
            if k == 0:
                made["east"] = made["west"] = moved
            made["east"] = jnp.where(group == k, moved, made["east"])
            made["west"] = jnp.where(group_west == k, moved, made["west"])
            if k == 4:
                wires[0, pl.ds(row, 8), :] = made["east"]
                wires[1, pl.ds(row, 8), :] = made["west"]

        staggered([(row, k) for row in starts for k in range(5)], (move, merge, send), 3)

    def wire_copies(start, count, number):
        return [
            pltpu.make_async_remote_copy(
                wires.at[side, pl.ds(start, count)],
                wires_in.at[side, pl.ds(start, count)],
                wire_send.at[side, number],
                wire_recv.at[side, number],
                device_id=device,
                device_id_type=MESH,
            )
            for side, device in ((0, east), (1, west))
        ]

    tiles = rows // 8

    @pl.loop(0, CHUNKS)
    def _(chunk):
        for copy in loads(chunk):
            copy.wait()
        first = pl.multiple_of(part * chunk, 8)
        for layer in range(layers):
            for half in range(2):
                wet = wet_int[layer, half, pl.ds(first, part), :]
                x0[4, layer, half, pl.ds(pl.multiple_of(first + 8, 8), part), :] = wet.astype(jnp.float32)
        pack_tiles([pl.multiple_of(first + 8 + 8 * j, 8) for j in range(part // 8)])

    def loader(source, layer, first):
        def load(k, offset):
            at = pl.ds(first + offset, 8)
            return [(x0 if k == 4 else source)[k, layer, half, at, :] for half in range(2)]

        return load

    def face_weights(load, layer, first, first_step):
        at = pl.ds(first, 8)

        def faces(kept, make):
            if not first_step:
                return [kept[layer, half, at, :] for half in range(2)]
            values = make(load)
            for half in range(2):
                kept[layer, half, at, :] = values[half]
            return values

        return functools.partial(faces, east_wet, wet_east), functools.partial(faces, north_wet, wet_north)

    def whole_blocks(source, target, first_step, meanwhile):
        def tile(layer, first):
            at = pl.ds(first, 8)

            def south(k, flux):
                for half in range(2):
                    flows[k, half, at, :] = flux[half]
                return [flows[k, half, pl.ds(first - 1, 8), :] for half in range(2)]

            def put(k, new):
                for half in range(2):
                    target[k, layer, half, at, :] = new[half]

            load = loader(source, layer, first)
            return load, *face_weights(load, layer, first, first_step), south, put, False

        @pl.loop(0, layers)
        def _(layer):
            for before, function in meanwhile:
                pl.when(layer == before)(function)

            @pl.loop(0, rows // (8 * BLOCKS))
            def _(i):
                first = pl.multiple_of(8 + 8 * BLOCKS * i, 8)
                tiles_step([tile(layer, pl.multiple_of(first + 8 * j, 8)) for j in range(BLOCKS)], 12)

    sublane = lax.broadcasted_iota(jnp.int32, (8, 128), 0)

    def edge_rows(source, target, starts, first_step):
        right = jnp.logical_and(sublane >= 2, sublane < 6)

        def tile(layer, first):
            at = pl.ds(first, 8)

            def put(k, new):
                for half in range(2):
                    target[k, layer, half, at, :] = jnp.where(right, new[half], target[k, layer, half, at, :])

            load = loader(source, layer, first)
            return load, *face_weights(load, layer, first, first_step), rolled_south, put, False

        @pl.loop(0, layers // EDGES)
        def _(i):
            tiles_step([tile(EDGES * i + j, first) for j in range(EDGES) for first in starts], 12)

    past_fold = jnp.logical_and(sublane >= 4, sublane < 6)

    def fold_rows():
        first = north_pad - 4

        def tile(layer):
            at = pl.ds(first, 8)

            def put(k, new):
                for half in range(2):
                    x1[k, layer, half, at, :] = jnp.where(past_fold, new[half], x1[k, layer, half, at, :])

            load = loader(x0, layer, first)
            return load, lambda: wet_east(load), lambda: wet_north(load), rolled_south, put, True

        tiles_step([tile(layer) for layer in range(layers)], 12)

    def send_edges():
        @pl.when(bottom)
        def _():
            pl.semaphore_wait(barrier, 3)

        @pl.when(jnp.logical_not(bottom))
        def _():
            pl.semaphore_wait(barrier, 4)

        @pl.when(top)
        def _():
            for copy in to_mirror:
                copy.start()

        @pl.when(jnp.logical_not(top))
        def _():
            for copy in to_north:
                copy.start()

        @pl.when(jnp.logical_not(bottom))
        def _():
            for copy in to_south:
                copy.start()

        for copy in wire_copies(8, rows, 0):
            copy.start()

    whole_blocks(x0, x1, True, [(EARLY, send_edges)])

    @pl.when(bottom)
    def _():
        @pl.loop(0, layers)
        def _(layer):
            for half in range(2):
                for k in range(5):
                    x0[k, layer, half, pl.ds(0, 8), :] = jnp.zeros((8, 128), jnp.float32)

    @pl.when(jnp.logical_not(bottom))
    def _():
        for copy in row_copies(0, 4, 0, east):
            copy.wait_recv()

        @pl.loop(0, layers)
        def _(layer):
            for half in range(2):
                for k in range(4):
                    x0[k, layer, half, pl.ds(0, 8), :] = rows_in[0, k, layer, half]
                x0[4, layer, half, pl.ds(0, 8), :] = wet_rows_in[0, layer, half].astype(jnp.float32)

    def send_corner(number, start):
        pack_tiles([start])
        for copy in wire_copies(start, 8, number):
            copy.start()

    send_corner(1, 0)

    def north_tile(k, layer, half):
        return wet_rows_in[1, layer, half].astype(jnp.float32) if k == 4 else rows_in[1, k, layer, half]

    @pl.when(jnp.logical_not(top))
    def _():
        for copy in to_south:
            copy.wait_recv()

        @pl.loop(0, layers)
        def _(layer):
            for half in range(2):
                for k in range(5):
                    x0[k, layer, half, pl.ds(north_pad, 8), :] = north_tile(k, layer, half)

        send_corner(2, north_pad)

    def fold_halo():
        @pl.when(top)
        def _():
            for copy in to_south:
                copy.wait_recv()

            @pl.loop(0, layers)
            def _(layer):
                for half in range(2):
                    for k in range(5):
                        flipped = jnp.take_along_axis(north_tile(k, layer, 1 - half), 127 - lanes(), axis=1)
                        if k in (2, 3):
                            flipped = -flipped
                        for row in range(4):
                            x0[k, layer, half, pl.ds(north_pad + row, 1), :] = flipped[7 - row : 8 - row, :]

            send_corner(2, north_pad)

    whole_blocks(x1, out, False, [(MIDDLE, fold_halo)])
    wire_parts = wire_copies(8, rows, 0) + wire_copies(0, 8, 1) + wire_copies(north_pad, 8, 2)
    edge_rows(x0, x1, (4, north_pad - 4), True)
    pl.when(top)(fold_rows)
    edge_rows(x1, out, (6, north_pad - 6), False)

    def every_tile(*stages):
        @pl.loop(0, (tiles + 2) // JOINED)
        def _(i):
            at = [pl.ds(pl.multiple_of(8 * JOINED * i + 8 * j, 8), 8) for j in range(JOINED)]
            staggered([(tile, k) for tile in at for k in range(5)], stages, 8)

    def move_next(item, _):
        tile, k = item
        source = x0 if k == 4 else x1
        return pack_moves(lambda layer, half: source[k, layer, half, tile, :])

    def merge_next(item, moves):
        tile, k = item
        packed_next[k, tile, :] = pack(moves)

    every_tile(move_next, merge_next)

    for copy in wire_parts:
        copy.wait_recv()

    def join(item, _):
        tile, k = item
        own = packed[k, tile, :]
        return roll(wires_in[0, tile, :], -4 * k), own, roll(own, 8), roll(wires_in[1, tile, :], 8 - 4 * k)

    def select(parts):
        place = spot()
        left = jnp.where(place < 4, parts[0], parts[1])
        right = jnp.where(place < 12, parts[2], parts[3])
        return jnp.where(place < 8, left, right)

    def put_strip(item, parts):
        tile, k = item
        strip[k, tile, :] = select(parts)

    every_tile(join, put_strip)

    def strip_tile(source, first, put, south=None, late=False):
        def load(k, offset):
            return [source[k, pl.ds(first + offset, 8), :]]

        def stored(k, flux):
            strip_flows[k, pl.ds(first, 8), :] = flux[0]
            return [strip_flows[k, pl.ds(first - 1, 8), :]]

        made = lambda: wet_east(load), lambda: wet_north(load)
        return load, *made, south or stored, functools.partial(put, first), late

    def strip_step(source, put):
        @pl.loop(0, (tiles + 1) // STRIPS)
        def _(i):
            first = 4 + 8 * STRIPS * i
            tiles_step([strip_tile(source, first + 8 * j, put) for j in range(STRIPS)], 20)

    def put_mid(first, k, new):
        strip_mid[k, pl.ds(first, 8), :] = new[0]

    strip_step(strip, put_mid)

    @pl.when(top)
    def _():
        def put(first, k, new):
            at = pl.ds(first, 8)
            strip_mid[k, at, :] = jnp.where(past_fold, new[0], strip_mid[k, at, :])

        tiles_step([strip_tile(strip, north_pad - 4, put, rolled_south, True)], 4)

    def join_next(item, _):
        tile, k = item
        outer = strip[4, tile, :] if k == 4 else strip_mid[k, tile, :]
        inner = packed_next[k, tile, :]
        return roll(outer, -2), roll(inner, -2), roll(inner, 10), roll(outer, 2)

    def put_strip_next(item, parts):
        tile, k = item
        strip_next[k, tile, :] = select(parts)

    every_tile(join_next, put_strip_next)

    def put_out(first, k, new):
        place = spot()
        inside = jnp.logical_and(place >= 2, place < 6)
        strips_out[k, pl.ds(first, 8), :] = jnp.where(inside, new[0], roll(new[0], -12))

    strip_step(strip_next, put_out)

    for copy in wire_parts:
        copy.wait_send()
    for copy in to_mirror:
        copy.wait_send()

    @pl.when(jnp.logical_not(bottom))
    def _():
        for copy in to_south:
            copy.wait_send()


def write_kernel(blocks, strips, t_out, s_out, u_out, v_out, whole, sem):
    layers, rows, _ = t_out.shape
    copies = []
    for k, output in enumerate((t_out, s_out, u_out, v_out)):

        @pl.loop(0, rows // (8 * WRITTEN))
        def _(i):
            first = pl.multiple_of(8 * WRITTEN * i, 8)

            def move(start, _):
                strip = strips[k, pl.ds(start + 8, 8), :]
                return [roll(strip, 2 - PITCH * layer) for layer in range(layers)]

            def merge(start, moved):
                for layer in range(layers):
                    for half in range(2):
                        edge = lanes() < 4 if half == 0 else lanes() >= 124
                        block = blocks[k, layer, half, pl.ds(start + 8, 8), :]
                        whole[k, layer, half, pl.ds(start, 8), :] = jnp.where(edge, moved[layer], block)

            staggered([pl.multiple_of(first + 8 * j, 8) for j in range(WRITTEN)], (move, merge), 5)

        for layer in range(layers):
            for half in range(2):
                there = output.at[layer, :, pl.ds(128 * half, 128)]
                copy = pltpu.make_async_copy(whole.at[k, layer, half], there, sem.at[k, layer, half])
                copy.start()
                copies.append(copy)
    for copy in copies:
        copy.wait()


def local(lon_count, lat_count, *arrays):
    layers, rows, columns = arrays[0].shape
    padded = rows + 16
    vmem = pl.BlockSpec(memory_space=pltpu.VMEM)
    anywhere = pl.BlockSpec(memory_space=pltpu.HBM)
    dma = pltpu.SemaphoreType.DMA
    f32 = jnp.float32
    blocks, strips = pl.pallas_call(
        functools.partial(advance_kernel, lon_count, lat_count),
        name="advance",
        out_shape=(
            jax.ShapeDtypeStruct((4, layers, 2, padded, 128), f32),
            jax.ShapeDtypeStruct((4, padded, 128), f32),
        ),
        in_specs=[anywhere] * 5,
        out_specs=(vmem, vmem),
        scratch_shapes=[
            pltpu.VMEM((5, layers, 2, padded, 128), f32),
            pltpu.VMEM((4, layers, 2, padded, 128), f32),
            pltpu.VMEM((layers, 2, rows, 128), jnp.int32),
            pltpu.VMEM((layers, 2, padded, 128), f32),
            pltpu.VMEM((layers, 2, padded, 128), f32),
            pltpu.VMEM((2, 4, layers, 2, 8, 128), f32),
            pltpu.VMEM((2, layers, 2, 8, 128), jnp.int32),
            pltpu.VMEM((5, padded, 128), f32),
            pltpu.VMEM((5, padded, 128), f32),
            pltpu.VMEM((2, padded, 128), f32),
            pltpu.VMEM((2, padded, 128), f32),
            pltpu.VMEM((5, padded, 128), f32),
            pltpu.VMEM((4, padded, 128), f32),
            pltpu.VMEM((5, padded, 128), f32),
            pltpu.VMEM((4, 2, padded, 128), f32),
            pltpu.VMEM((4, padded, 128), f32),
            dma((CHUNKS, 5, 2)),
            dma((2, 5, 2)),
            dma((2, 5, 2)),
            dma((2, 3)),
            dma((2, 3)),
        ],
        compiler_params=pltpu.CompilerParams(collective_id=0, has_side_effects=True, vmem_limit_bytes=40 << 20),
    )(*(pltpu.with_memory_space_constraint(array, pltpu.HBM) for array in arrays))
    return pl.pallas_call(
        write_kernel,
        name="write",
        out_shape=tuple(jax.ShapeDtypeStruct((layers, rows, columns), f32) for _ in range(4)),
        in_specs=[vmem, vmem],
        out_specs=(anywhere,) * 4,
        scratch_shapes=[pltpu.VMEM((4, layers, 2, rows, 128), f32), dma((4, layers, 2))],
        compiler_params=pltpu.CompilerParams(vmem_limit_bytes=40 << 20),
    )(blocks, strips)


def solution(mesh):
    placed = P(None, "lat", "lon")
    return jax.shard_map(
        functools.partial(local, mesh.shape["lon"], mesh.shape["lat"]),
        mesh=mesh,
        in_specs=(placed,) * 5,
        out_specs=(placed,) * 4,
        check_vma=False,
    )
```

```python
import functools

import jax
import jax.numpy as jnp
from jax import lax
from jax.experimental import pallas as pl
from jax.experimental.pallas import tpu as pltpu
from jax.sharding import PartitionSpec as P

MESH = pl.DeviceIdType.MESH
SCALE = 0.2 / 6.0
PITCH = 20
CHUNKS = 4
EARLY = 1
LATER = 2
MIDDLE = 2
BLOCKS = 24
EDGES = 6
STRIPS = 25
JOINED = 13
WRITTEN = 12


def lanes():
    return lax.broadcasted_iota(jnp.int32, (8, 128), 1)


def spot():
    return lax.rem(lax.rem(lanes() + 4, 128), PITCH)


def roll(x, shift):
    shift = shift % 128 if isinstance(shift, int) else shift
    return x if isinstance(shift, int) and shift == 0 else pltpu.roll(x, shift, 1)


def shifted(values, distance):
    moved = [roll(value, -distance) for value in values]
    if len(moved) == 1:
        return moved
    first, second = moved
    if distance > 0:
        return [jnp.where(lanes() < 128 - distance, first, second), second]
    return [first, jnp.where(lanes() >= -distance, second, first)]


def face(weight, positive, before, here, after, beyond):
    near = jnp.where(positive, here, after)
    far = jnp.where(positive, before, beyond)
    return weight * (2.0 * (here + after) + (3.0 * near - far))


def staggered(items, stages, lag):
    held = [None] * len(items)
    for step in range(len(items) + lag * (len(stages) - 1)):
        for number, stage in enumerate(stages):
            at = step - lag * number
            if 0 <= at < len(items):
                held[at] = stage(items[at], held[at])


def tiles_step(tiles, lag):
    made = {}

    def shifts(item, _):
        number, k = item
        load, east_faces, _, _, _, late = tiles[number]
        here = load(k, 0)
        fields = shifted(here, -1), here, shifted(here, 1), shifted(here, 2)
        if k == 0:
            made[number, 0] = east_faces()
        if k == 2:
            made[number, 2] = fields[2] if late else here
        return fields

    def east(item, fields):
        number, k = item
        if k == 0:
            weight = [q * s for q, s in zip(made[number, 2], made[number, 0])]
            made[number, 0] = weight, [q > 0.0 for q in weight]
        flux = [face(*values) for values in zip(*made[number, 0], *fields)]
        return flux, shifted(flux, -1)

    def north(item, changes):
        number, k = item
        load, _, north_faces, south, put, late = tiles[number]
        if k == 0:
            weight = [q * s for q, s in zip(load(3, 1 if late else 0), north_faces())]
            made[number, 0] = weight, [q > 0.0 for q in weight]
        here = load(k, 0)
        flux = [face(*values) for values in zip(*made[number, 0], load(k, -1), here, load(k, 1), load(k, 2))]
        parts = zip(here, *changes, flux, south(k, flux), load(4, 0))
        put(k, [(q - ((e - w) + (n - m))) * s for q, e, w, n, m, s in parts])

    staggered([(number, k) for number in range(len(tiles)) for k in range(4)], (shifts, east, north), lag)


def rolled_south(k, flux):
    return [pltpu.roll(value, 1, 0) for value in flux]


def wet_east(load):
    here = load(4, 0)
    return [w * e * SCALE for w, e in zip(here, shifted(here, 1))]


def wet_north(load):
    return [w * n * SCALE for w, n in zip(load(4, 0), load(4, 1))]


def local_position():
    return lax.axis_index("lon"), lax.axis_index("lat")


def advance_kernel(
    lon_count,
    lat_count,
    t_ref,
    s_ref,
    u_ref,
    v_ref,
    w_ref,
    out,
    strips_out,
    x0,
    x1,
    wet_int,
    east_wet,
    north_wet,
    rows_in,
    wet_rows_in,
    packed,
    packed_next,
    wires,
    wires_in,
    strip,
    strip_mid,
    strip_next,
    flows,
    strip_flows,
    load_sem,
    row_send,
    row_recv,
    wire_send,
    wire_recv,
):
    inputs = (t_ref, s_ref, u_ref, v_ref, w_ref)
    layers, rows, _ = t_ref.shape
    north_pad = 8 + rows
    lon, lat = local_position()
    top = lat == lat_count - 1
    bottom = lat == 0
    east = {"lon": lax.rem(lon + 1, lon_count)}
    west = {"lon": lax.rem(lon + lon_count - 1, lon_count)}
    mirror = {"lon": lon_count - 1 - lon}

    part = rows // CHUNKS

    def loads(chunk):
        first = pl.multiple_of(part * chunk, 8)
        copies = []
        for k in (4, 0, 1, 2, 3):
            for half in range(2):
                here = inputs[k].at[:, pl.ds(first, part), pl.ds(128 * half, 128)]
                if k == 4:
                    there = wet_int.at[:, half, pl.ds(first, part)]
                else:
                    there = x0.at[k, :, half, pl.ds(pl.multiple_of(first + 8, 8), part)]
                copies.append(pltpu.make_async_copy(here, there, load_sem.at[chunk, k, half]))
        return copies

    @pl.loop(0, CHUNKS)
    def _(chunk):
        for copy in loads(chunk):
            copy.start()

    barrier = pltpu.get_barrier_semaphore()
    pl.semaphore_signal(barrier, inc=1, device_id=east, device_id_type=MESH)
    pl.semaphore_signal(barrier, inc=1, device_id=west, device_id_type=MESH)

    @pl.when(top)
    def _():
        pl.semaphore_signal(barrier, inc=1, device_id=mirror, device_id_type=MESH)

    @pl.when(jnp.logical_not(top))
    def _():
        pl.semaphore_signal(barrier, inc=1, device_id={"lat": lat + 1}, device_id_type=MESH)

    @pl.when(jnp.logical_not(bottom))
    def _():
        pl.semaphore_signal(barrier, inc=1, device_id={"lat": lat - 1}, device_id_type=MESH)

    def row_copies(first, there, side, device):
        copies = []
        for k in range(5):
            for half in range(2):
                source = inputs[k].at[:, pl.ds(first, 4), pl.ds(128 * half, 128)]
                if k == 4:
                    target = wet_rows_in.at[side, :, half, pl.ds(there, 4)]
                else:
                    target = rows_in.at[side, k, :, half, pl.ds(there, 4)]
                up = 0 if first else 1
                copies.append(
                    pltpu.make_async_remote_copy(
                        source,
                        target,
                        row_send.at[up, k, half],
                        row_recv.at[side, k, half],
                        device_id=device,
                        device_id_type=MESH,
                    )
                )
        return copies

    to_north = row_copies(rows - 4, 4, 0, {"lat": jnp.minimum(lat + 1, lat_count - 1)})
    to_mirror = row_copies(rows - 4, 4, 1, mirror)
    to_south = row_copies(0, 0, 1, {"lat": jnp.maximum(lat - 1, 0)})

    def pack_moves(source):
        return [roll(jnp.where(lanes() < 64, source(layer, 0), source(layer, 1)), PITCH * layer) for layer in range(layers)]

    def pack(moves):
        place = lax.rem(lanes() + 4, 128)
        total = moves[-1]
        for layer in reversed(range(layers - 1)):
            total = jnp.where(place < PITCH * (layer + 1) - 6, moves[layer], total)
        return jnp.where(place < 120, total, moves[0])

    def pack_tiles(starts):
        group = spot() // 4
        group_west = lax.rem(lanes(), PITCH) // 4
        made = {}

        def move(item, _):
            row, k = item
            return pack_moves(lambda layer, half: x0[k, layer, half, pl.ds(row, 8), :])

        def merge(item, moves):
            row, k = item
            one = pack(moves)
            packed[k, pl.ds(row, 8), :] = one
            return roll(one, 4 * k)

        def send(item, moved):
            row, k = item
            if k == 0:
                made["east"] = made["west"] = moved
            made["east"] = jnp.where(group == k, moved, made["east"])
            made["west"] = jnp.where(group_west == k, moved, made["west"])
            if k == 4:
                wires[0, pl.ds(row, 8), :] = made["east"]
                wires[1, pl.ds(row, 8), :] = made["west"]

        staggered([(row, k) for row in starts for k in range(5)], (move, merge, send), 3)

    def wire_copies(start, count, number):
        return [
            pltpu.make_async_remote_copy(
                wires.at[side, pl.ds(start, count)],
                wires_in.at[side, pl.ds(start, count)],
                wire_send.at[side, number],
                wire_recv.at[side, number],
                device_id=device,
                device_id_type=MESH,
            )
            for side, device in ((0, east), (1, west))
        ]

    tiles = rows // 8

    @pl.loop(0, CHUNKS)
    def _(chunk):
        for copy in loads(chunk):
            copy.wait()
        first = pl.multiple_of(part * chunk, 8)
        for layer in range(layers):
            for half in range(2):
                wet = wet_int[layer, half, pl.ds(first, part), :]
                x0[4, layer, half, pl.ds(pl.multiple_of(first + 8, 8), part), :] = wet.astype(jnp.float32)
        pack_tiles([pl.multiple_of(first + 8 + 8 * j, 8) for j in range(part // 8)])

    def loader(source, layer, first):
        def load(k, offset):
            at = pl.ds(first + offset, 8)
            return [(x0 if k == 4 else source)[k, layer, half, at, :] for half in range(2)]

        return load

    def face_weights(load, layer, first, first_step):
        at = pl.ds(first, 8)

        def faces(kept, make):
            if not first_step:
                return [kept[layer, half, at, :] for half in range(2)]
            values = make(load)
            for half in range(2):
                kept[layer, half, at, :] = values[half]
            return values

        return functools.partial(faces, east_wet, wet_east), functools.partial(faces, north_wet, wet_north)

    def whole_blocks(source, target, first_step, meanwhile):
        def tile(layer, first):
            at = pl.ds(first, 8)

            def south(k, flux):
                for half in range(2):
                    flows[k, half, at, :] = flux[half]
                return [flows[k, half, pl.ds(first - 1, 8), :] for half in range(2)]

            def put(k, new):
                for half in range(2):
                    target[k, layer, half, at, :] = new[half]

            load = loader(source, layer, first)
            return load, *face_weights(load, layer, first, first_step), south, put, False

        @pl.loop(0, layers)
        def _(layer):
            for before, function in meanwhile:
                pl.when(layer == before)(function)

            @pl.loop(0, rows // (8 * BLOCKS))
            def _(i):
                first = pl.multiple_of(8 + 8 * BLOCKS * i, 8)
                tiles_step([tile(layer, pl.multiple_of(first + 8 * j, 8)) for j in range(BLOCKS)], 12)

    sublane = lax.broadcasted_iota(jnp.int32, (8, 128), 0)

    def edge_rows(source, target, starts, first_step):
        right = jnp.logical_and(sublane >= 2, sublane < 6)

        def tile(layer, first):
            at = pl.ds(first, 8)

            def put(k, new):
                for half in range(2):
                    target[k, layer, half, at, :] = jnp.where(right, new[half], target[k, layer, half, at, :])

            load = loader(source, layer, first)
            return load, *face_weights(load, layer, first, first_step), rolled_south, put, False

        @pl.loop(0, layers // EDGES)
        def _(i):
            tiles_step([tile(EDGES * i + j, first) for j in range(EDGES) for first in starts], 12)

    past_fold = jnp.logical_and(sublane >= 4, sublane < 6)

    def fold_rows():
        first = north_pad - 4

        def tile(layer):
            at = pl.ds(first, 8)

            def put(k, new):
                for half in range(2):
                    x1[k, layer, half, at, :] = jnp.where(past_fold, new[half], x1[k, layer, half, at, :])

            load = loader(x0, layer, first)
            return load, lambda: wet_east(load), lambda: wet_north(load), rolled_south, put, True

        tiles_step([tile(layer) for layer in range(layers)], 12)

    def send_rows():
        @pl.when(bottom)
        def _():
            pl.semaphore_wait(barrier, 3)

        @pl.when(jnp.logical_not(bottom))
        def _():
            pl.semaphore_wait(barrier, 4)

        @pl.when(top)
        def _():
            for copy in to_mirror:
                copy.start()

        @pl.when(jnp.logical_not(top))
        def _():
            for copy in to_north:
                copy.start()

        @pl.when(jnp.logical_not(bottom))
        def _():
            for copy in to_south:
                copy.start()

    def send_wires():
        for copy in wire_copies(8, rows, 0):
            copy.start()

    whole_blocks(x0, x1, True, [(EARLY, send_rows), (LATER, send_wires)])

    @pl.when(bottom)
    def _():
        @pl.loop(0, layers)
        def _(layer):
            for half in range(2):
                for k in range(5):
                    x0[k, layer, half, pl.ds(0, 8), :] = jnp.zeros((8, 128), jnp.float32)

    @pl.when(jnp.logical_not(bottom))
    def _():
        for copy in row_copies(0, 4, 0, east):
            copy.wait_recv()

        @pl.loop(0, layers)
        def _(layer):
            for half in range(2):
                for k in range(4):
                    x0[k, layer, half, pl.ds(0, 8), :] = rows_in[0, k, layer, half]
                x0[4, layer, half, pl.ds(0, 8), :] = wet_rows_in[0, layer, half].astype(jnp.float32)

    def send_corner(number, start):
        pack_tiles([start])
        for copy in wire_copies(start, 8, number):
            copy.start()

    send_corner(1, 0)

    def north_tile(k, layer, half):
        return wet_rows_in[1, layer, half].astype(jnp.float32) if k == 4 else rows_in[1, k, layer, half]

    @pl.when(jnp.logical_not(top))
    def _():
        for copy in to_south:
            copy.wait_recv()

        @pl.loop(0, layers)
        def _(layer):
            for half in range(2):
                for k in range(5):
                    x0[k, layer, half, pl.ds(north_pad, 8), :] = north_tile(k, layer, half)

        send_corner(2, north_pad)

    def fold_halo():
        @pl.when(top)
        def _():
            for copy in to_south:
                copy.wait_recv()

            @pl.loop(0, layers)
            def _(layer):
                for half in range(2):
                    for k in range(5):
                        flipped = jnp.take_along_axis(north_tile(k, layer, 1 - half), 127 - lanes(), axis=1)
                        if k in (2, 3):
                            flipped = -flipped
                        for row in range(4):
                            x0[k, layer, half, pl.ds(north_pad + row, 1), :] = flipped[7 - row : 8 - row, :]

            send_corner(2, north_pad)

    whole_blocks(x1, out, False, [(MIDDLE, fold_halo)])
    wire_parts = wire_copies(8, rows, 0) + wire_copies(0, 8, 1) + wire_copies(north_pad, 8, 2)
    edge_rows(x0, x1, (4, north_pad - 4), True)
    pl.when(top)(fold_rows)
    edge_rows(x1, out, (6, north_pad - 6), False)

    def every_tile(*stages):
        @pl.loop(0, (tiles + 2) // JOINED)
        def _(i):
            at = [pl.ds(pl.multiple_of(8 * JOINED * i + 8 * j, 8), 8) for j in range(JOINED)]
            staggered([(tile, k) for tile in at for k in range(5)], stages, 8)

    def move_next(item, _):
        tile, k = item
        source = x0 if k == 4 else x1
        return pack_moves(lambda layer, half: source[k, layer, half, tile, :])

    def merge_next(item, moves):
        tile, k = item
        packed_next[k, tile, :] = pack(moves)

    every_tile(move_next, merge_next)

    for copy in wire_parts:
        copy.wait_recv()

    def join(item, _):
        tile, k = item
        own = packed[k, tile, :]
        return roll(wires_in[0, tile, :], -4 * k), own, roll(own, 8), roll(wires_in[1, tile, :], 8 - 4 * k)

    def select(parts):
        place = spot()
        left = jnp.where(place < 4, parts[0], parts[1])
        right = jnp.where(place < 12, parts[2], parts[3])
        return jnp.where(place < 8, left, right)

    def put_strip(item, parts):
        tile, k = item
        strip[k, tile, :] = select(parts)

    every_tile(join, put_strip)

    def strip_tile(source, first, put, south=None, late=False):
        def load(k, offset):
            return [source[k, pl.ds(first + offset, 8), :]]

        def stored(k, flux):
            strip_flows[k, pl.ds(first, 8), :] = flux[0]
            return [strip_flows[k, pl.ds(first - 1, 8), :]]

        made = lambda: wet_east(load), lambda: wet_north(load)
        return load, *made, south or stored, functools.partial(put, first), late

    def strip_step(source, put):
        @pl.loop(0, (tiles + 1) // STRIPS)
        def _(i):
            first = 4 + 8 * STRIPS * i
            tiles_step([strip_tile(source, first + 8 * j, put) for j in range(STRIPS)], 20)

    def put_mid(first, k, new):
        strip_mid[k, pl.ds(first, 8), :] = new[0]

    strip_step(strip, put_mid)

    @pl.when(top)
    def _():
        def put(first, k, new):
            at = pl.ds(first, 8)
            strip_mid[k, at, :] = jnp.where(past_fold, new[0], strip_mid[k, at, :])

        tiles_step([strip_tile(strip, north_pad - 4, put, rolled_south, True)], 4)

    def join_next(item, _):
        tile, k = item
        outer = strip[4, tile, :] if k == 4 else strip_mid[k, tile, :]
        inner = packed_next[k, tile, :]
        return roll(outer, -2), roll(inner, -2), roll(inner, 10), roll(outer, 2)

    def put_strip_next(item, parts):
        tile, k = item
        strip_next[k, tile, :] = select(parts)

    every_tile(join_next, put_strip_next)

    def put_out(first, k, new):
        place = spot()
        inside = jnp.logical_and(place >= 2, place < 6)
        strips_out[k, pl.ds(first, 8), :] = jnp.where(inside, new[0], roll(new[0], -12))

    strip_step(strip_next, put_out)

    for copy in wire_parts:
        copy.wait_send()
    for copy in to_mirror:
        copy.wait_send()

    @pl.when(jnp.logical_not(bottom))
    def _():
        for copy in to_south:
            copy.wait_send()


def write_kernel(blocks, strips, t_out, s_out, u_out, v_out, whole, sem):
    layers, rows, _ = t_out.shape
    copies = []
    for k, output in enumerate((t_out, s_out, u_out, v_out)):

        @pl.loop(0, rows // (8 * WRITTEN))
        def _(i):
            first = pl.multiple_of(8 * WRITTEN * i, 8)

            def move(start, _):
                strip = strips[k, pl.ds(start + 8, 8), :]
                return [roll(strip, 2 - PITCH * layer) for layer in range(layers)]

            def merge(start, moved):
                for layer in range(layers):
                    for half in range(2):
                        edge = lanes() < 4 if half == 0 else lanes() >= 124
                        block = blocks[k, layer, half, pl.ds(start + 8, 8), :]
                        whole[k, layer, half, pl.ds(start, 8), :] = jnp.where(edge, moved[layer], block)

            staggered([pl.multiple_of(first + 8 * j, 8) for j in range(WRITTEN)], (move, merge), 5)

        for layer in range(layers):
            for half in range(2):
                there = output.at[layer, :, pl.ds(128 * half, 128)]
                copy = pltpu.make_async_copy(whole.at[k, layer, half], there, sem.at[k, layer, half])
                copy.start()
                copies.append(copy)
    for copy in copies:
        copy.wait()


def local(lon_count, lat_count, *arrays):
    layers, rows, columns = arrays[0].shape
    padded = rows + 16
    vmem = pl.BlockSpec(memory_space=pltpu.VMEM)
    anywhere = pl.BlockSpec(memory_space=pltpu.HBM)
    dma = pltpu.SemaphoreType.DMA
    f32 = jnp.float32
    blocks, strips = pl.pallas_call(
        functools.partial(advance_kernel, lon_count, lat_count),
        name="advance",
        out_shape=(
            jax.ShapeDtypeStruct((4, layers, 2, padded, 128), f32),
            jax.ShapeDtypeStruct((4, padded, 128), f32),
        ),
        in_specs=[anywhere] * 5,
        out_specs=(vmem, vmem),
        scratch_shapes=[
            pltpu.VMEM((5, layers, 2, padded, 128), f32),
            pltpu.VMEM((4, layers, 2, padded, 128), f32),
            pltpu.VMEM((layers, 2, rows, 128), jnp.int32),
            pltpu.VMEM((layers, 2, padded, 128), f32),
            pltpu.VMEM((layers, 2, padded, 128), f32),
            pltpu.VMEM((2, 4, layers, 2, 8, 128), f32),
            pltpu.VMEM((2, layers, 2, 8, 128), jnp.int32),
            pltpu.VMEM((5, padded, 128), f32),
            pltpu.VMEM((5, padded, 128), f32),
            pltpu.VMEM((2, padded, 128), f32),
            pltpu.VMEM((2, padded, 128), f32),
            pltpu.VMEM((5, padded, 128), f32),
            pltpu.VMEM((4, padded, 128), f32),
            pltpu.VMEM((5, padded, 128), f32),
            pltpu.VMEM((4, 2, padded, 128), f32),
            pltpu.VMEM((4, padded, 128), f32),
            dma((CHUNKS, 5, 2)),
            dma((2, 5, 2)),
            dma((2, 5, 2)),
            dma((2, 3)),
            dma((2, 3)),
        ],
        compiler_params=pltpu.CompilerParams(collective_id=0, has_side_effects=True, vmem_limit_bytes=40 << 20),
    )(*(pltpu.with_memory_space_constraint(array, pltpu.HBM) for array in arrays))
    return pl.pallas_call(
        write_kernel,
        name="write",
        out_shape=tuple(jax.ShapeDtypeStruct((layers, rows, columns), f32) for _ in range(4)),
        in_specs=[vmem, vmem],
        out_specs=(anywhere,) * 4,
        scratch_shapes=[pltpu.VMEM((4, layers, 2, rows, 128), f32), dma((4, layers, 2))],
        compiler_params=pltpu.CompilerParams(vmem_limit_bytes=40 << 20),
    )(blocks, strips)


def solution(mesh):
    placed = P(None, "lat", "lon")
    return jax.shard_map(
        functools.partial(local, mesh.shape["lon"], mesh.shape["lat"]),
        mesh=mesh,
        in_specs=(placed,) * 5,
        out_specs=(placed,) * 4,
        check_vma=False,
    )
```
